32 devices in a mesh: groups: 2 (over y), ctx: 4 (over z), head: 2 (over x), pair: 2 (over core).
Axes of the slice: x: 2, y: 2, z: 4, core: 2. Of those that a mesh axis runs over, the one named last changes fastest.
Arguments:
- queries: bfloat16 [64, 32, 128], P('groups', 'head'), parts along dimension 0, may hold values from -80 to 80
- prompt_keys: bfloat16 [32768, 4, 128], P(('groups', 'ctx', 'pair'), 'head'), parts along dimension 0, may hold values from -32 to 32
- prompt_values: bfloat16 [32768, 4, 128], P(('groups', 'ctx', 'pair'), 'head'), parts along dimension 0, may hold values from -6 to 6
- residual: bfloat16 [64, 2048], P(('groups', 'ctx', 'head', 'pair')), parts along dimension 0, may hold values from -0.59765625 to 0.59765625
- out_weight: bfloat16 [4096, 2048], P('head', 'ctx'), may hold values from -0.09375 to 0.09375
- norm_gain: float32 [2048], replicated, may hold values from 0.1 to 1.9
- expert_lists: int32 [64, 8], P(('groups', 'ctx')), parts along dimension 0, may hold values from 0 to 15, all different within a row; in each aligned block of 8 rows (0 to 7, 8 to 15, ...) at most 8 rows name the same one
- gate_weights: float32 [64, 8], P(('groups', 'ctx')), parts along dimension 0, may hold values from 0.05 to 0.4
- gate_up: bfloat16 [16, 2048, 1536], P(('ctx', 'head', 'pair')), may hold values from -0.125 to 0.125
- down_proj: bfloat16 [16, 768, 2048], P(('ctx', 'head', 'pair')), may hold values from -0.21875 to 0.21875
Outputs:
- layer_out: bfloat16 [64, 2048], P(('groups', 'ctx', 'head', 'pair')), parts along dimension 0
The draws below stay inside these ranges and needn't reach their ends.
There are 2 independent parts, one for each index of `groups`. The reference program is written for one: setup_inputs(seed, part) draws one part's arguments, and reference() takes and returns one part's arrays. A program takes and returns all parts, laid end to end along the dimension named above; an argument that names none is the same for every part. Nothing has to cross between parts.
Inputs may be any that keep to these rules, and one draw needn't show every extreme that they name: `expert_lists`: A row names 8 different experts. In each aligned block of 8 rows (the rows of one index of ctx) no expert is named by more than 8 rows.
All inputs are finite; a program needn't handle non-finite values.
Results may differ from the reference program's by a relative error of at most 0.018.
Values may be sent and summed in bfloat16 or wider, within the bound.
A program may use at most 128 MiB of HBM per device.

```python
import math
import jax
import jax.numpy as jnp
import numpy as np
from jax import lax

D = 2048
HEADS = 32
KVH = 4
HD = 128
FFE = 768
TOP = 8
EXPERTS = 16
ROWS = 32
LEN = 16384
ROWS_BLK = 8
CAP = 8


def shared_attention(key):
    position = jnp.arange(LEN, dtype=jnp.float32) / LEN
    base = jnp.clip(jax.random.normal(jax.random.fold_in(key, 101), (LEN, KVH, HD), jnp.float32), -6.0, 6.0)
    queries = jnp.clip(jax.random.normal(jax.random.fold_in(key, 102), (ROWS, HEADS, HD), jnp.float32), -6.0, 6.0)
    keys_out = base * (2.1 + 0.6 * position)[:, None, None]
    return (queries, keys_out)


def draw_queries(key, part):
    return shared_attention(key)[0].astype(jnp.bfloat16)


def draw_prompt_keys(key, part):
    return shared_attention(key)[1].astype(jnp.bfloat16)


def block_scale(stream_key, dims, shards, smallest, largest):
    def one(dim, parts):
        draws = jax.random.uniform(jax.random.fold_in(jax.random.fold_in(stream_key, 6), dim), (parts,), jnp.float32, smallest / len(shards), largest / len(shards))
        return jnp.repeat(jnp.exp(draws), dims[dim] // parts).reshape((-1,) + (1,) * (len(dims) - dim - 1))

    loudness = one(*shards[0])
    for cut in shards[1:]:
        loudness = loudness * one(*cut)
    return loudness


def routed_block(stream_key, own, number, rows, count, top, bound, skew):
    ranking = jax.random.permutation(stream_key, count)
    crowded, usual = load_shares(count, rows * top, bound, skew, True), load_shares(count, rows * top, bound, skew, False)
    places = jnp.arange(count)

    def named(lengths, rotation):
        used = int((lengths > 0).sum())
        fixed = max(1, used // 4)
        passed = fixed + (places - fixed + rotation * (used - fixed)) % max(1, count - fixed)
        return jnp.zeros((count,), jnp.int32).at[ranking[jnp.where(places < fixed, places, passed)]].set(jnp.asarray(lengths, jnp.int32))

    lengths = jnp.where(number % 4 == 0, named(crowded, number // 4), named(usual, number - number // 4 - 1))
    mixed = jax.random.permutation(jax.random.fold_in(own, 3), count)
    source_of, receiver = mixed[0:count // 2 * 2:2], mixed[1:count // 2 * 2:2]
    room = jnp.minimum(lengths[source_of] - 1, bound - lengths[receiver]) // 2
    room = jnp.where((source_of == ranking[0]) | (receiver == ranking[0]) | (lengths[receiver] == 0), 0, jnp.maximum(room, 0))
    passed = jax.random.randint(jax.random.fold_in(own, 4), (count // 2,), 0, 1 << 20) % (room + 1)
    lengths = lengths.at[source_of].add(-passed).at[receiver].add(passed)
    members = jnp.searchsorted(jnp.cumsum(lengths), jnp.arange(rows * top), side="right").astype(jnp.int32)
    table = members.reshape(top, rows).T
    table = table[jax.random.permutation(jax.random.fold_in(own, 1), rows)]
    rotation = jax.random.randint(jax.random.fold_in(own, 2), (rows, 1), 0, top)
    return jnp.take_along_axis(table, (jnp.arange(top)[None, :] + rotation) % top, axis=1)


def load_shares(amount, total, most, skew, full):
    loads = [(1 << 20) // math.isqrt(rank ** skew) + 1 for rank in range(1, amount + 1)]
    largest = most if full else min(most, max(-(-total // amount), total * loads[0] // sum(loads)))
    least = 1 if total - largest >= amount - 1 else 0
    counts, rest = [largest] + [least] * (amount - 1), total - largest - least * (amount - 1)
    while rest > 0:
        free = [i for i in range(1, amount) if counts[i] < largest] or [i for i in range(1, amount) if counts[i] < most]
        mass, left = sum([loads[i] for i in free]), rest
        for i in free:
            addition = min(most - counts[i], max(1, left * loads[i] // mass), rest)
            counts[i] = counts[i] + addition
            rest = rest - addition
    return np.array(counts)


def gaussian(key, extent, scale, bound, cuts=(), held_as=jnp.bfloat16):
    values = jax.random.normal(key, extent, jnp.float32) * scale
    if len(cuts) > 0:
        values = block_scale(key, extent, cuts, -0.22, 0.18) * values
    return jnp.clip(values, min=-bound, max=bound).astype(held_as)


def setup_inputs(seed: int = 0, part: int = 0) -> dict:
    key_list = jax.random.split(jax.random.key(seed), 11)
    part_keys = jax.random.split(jax.random.fold_in(key_list[10], part), 11)
    queries = draw_queries(jax.random.fold_in(jax.random.fold_in(key_list[10], part), 71), part)
    prompt_keys = draw_prompt_keys(jax.random.fold_in(jax.random.fold_in(key_list[10], part), 71), part)
    prompt_values = gaussian(part_keys[2], (LEN, KVH, HD), 1.0, 6.0, ((0, 8), (1, 2)))
    residual = gaussian(part_keys[3], (ROWS, D), 0.1, 0.59765625, ((0, 16),))
    out_weight = gaussian(key_list[4], (HEADS * HD, D), (HEADS * HD) ** -0.5, 0.09375, ((0, 2), (1, 4)))
    norm_gain = jnp.clip(1.0 + 0.18 * jax.random.normal(key_list[5], (D,), jnp.float32), 0.1, 1.9)
    expert_lists_keys = jax.random.split(jax.random.fold_in(part_keys[6], 1), ROWS // ROWS_BLK)
    expert_lists_turns = jax.random.permutation(jax.random.fold_in(part_keys[6], 3), ROWS // ROWS_BLK)
    expert_lists = jax.vmap(lambda own, number: routed_block(jax.random.fold_in(part_keys[6], 2), own, number, ROWS_BLK, EXPERTS, TOP, CAP, 2))(expert_lists_keys, expert_lists_turns).reshape((ROWS, TOP))
    gate_weights = jnp.clip(0.05 + 0.35 * jax.random.uniform(part_keys[7], (ROWS, TOP), jnp.float32) ** block_scale(part_keys[7], (ROWS, TOP), ((0, 4),), -0.2, 0.2), 0.05, 0.4)
    gate_up = gaussian(key_list[8], (EXPERTS, D, 2 * FFE), D ** -0.5, 0.125, ((0, 16),))
    down_proj = gaussian(key_list[9], (EXPERTS, FFE, D), FFE ** -0.5, 0.21875, ((0, 16),))
    return dict(queries=queries, prompt_keys=prompt_keys, prompt_values=prompt_values, residual=residual, out_weight=out_weight, norm_gain=norm_gain, expert_lists=expert_lists, gate_weights=gate_weights, gate_up=gate_up, down_proj=down_proj)


def attend(queries, prompt_keys, prompt_values):
    rows_all = queries.shape[0]
    group = HEADS // KVH
    block = min(1024, LEN)
    scale_factor = 1.0 / math.sqrt(HD)

    def per_head(index):
        query_rows = lax.dynamic_slice_in_dim(queries, index * group, group, 1).reshape(rows_all * group, HD)
        key_head = lax.dynamic_index_in_dim(prompt_keys, index, 1, keepdims=False)
        value_head = lax.dynamic_index_in_dim(prompt_values, index, 1, keepdims=False)
        key_blocks = key_head.reshape(LEN // block, block, HD)
        value_blocks = value_head.reshape(LEN // block, block, HD)

        def step(carry, pieces):
            running, total, numer = carry
            key_piece, value_piece = pieces
            scores = jnp.dot(query_rows, key_piece.T, preferred_element_type=jnp.float32) * scale_factor
            fresh = jnp.maximum(running, lax.optimization_barrier(jnp.max(scores, axis=1)))
            decay = jnp.exp(running - fresh)
            weights = jnp.exp(scores - fresh[:, None])
            total = total * decay + lax.optimization_barrier(jnp.sum(weights, axis=1))
            numer = numer * decay[:, None] + jnp.dot(weights.astype(jnp.bfloat16), value_piece, preferred_element_type=jnp.float32)
            return ((fresh, total, numer), None)
        count = rows_all * group
        start = (jnp.full((count,), -jnp.inf, jnp.float32), jnp.zeros((count,), jnp.float32), jnp.zeros((count, HD), jnp.float32))
        (running, total, numer), unused = lax.scan(step, start, (key_blocks, value_blocks))
        return (numer / total[:, None]).reshape(rows_all, group, HD)
    outputs = lax.map(per_head, jnp.arange(KVH, dtype=jnp.int32))
    return jnp.transpose(outputs, (1, 0, 2, 3)).reshape(rows_all, HEADS * HD)

def expert_apply(inputs, weight_both, weight_down):
    both = jnp.dot(inputs, weight_both, preferred_element_type=jnp.float32)
    inner = (jax.nn.silu(both[:, :FFE]) * both[:, FFE:]).astype(jnp.bfloat16)
    return jnp.dot(inner, weight_down, preferred_element_type=jnp.float32).astype(jnp.bfloat16)

def reference(queries, prompt_keys, prompt_values, residual, out_weight, norm_gain, expert_lists, gate_weights, gate_up, down_proj):
    attended = attend(queries, prompt_keys, prompt_values).astype(jnp.bfloat16)
    projected = jnp.dot(attended, out_weight, preferred_element_type=jnp.float32)
    hidden_state = (residual.astype(jnp.float32) + projected).astype(jnp.bfloat16)
    as_float = hidden_state.astype(jnp.float32)
    normed = (as_float * lax.rsqrt(lax.optimization_barrier(jnp.mean(as_float * as_float, axis=1, keepdims=True)) + 1e-06) * norm_gain).astype(jnp.bfloat16)
    slots_most = ROWS // ROWS_BLK * CAP

    def per_expert(carry, index):
        hits = expert_lists == index
        weight_row = lax.optimization_barrier(jnp.sum(jnp.where(hits, gate_weights, jnp.zeros_like(gate_weights)), axis=1))
        chosen = jnp.any(hits, axis=1)
        picked = jnp.nonzero(chosen, size=slots_most, fill_value=0)[0].astype(jnp.int32)
        valid = jnp.arange(slots_most, dtype=jnp.int32) < jnp.sum(chosen.astype(jnp.int32))
        weight_both = lax.dynamic_index_in_dim(gate_up, index, 0, keepdims=False)
        weight_down = lax.dynamic_index_in_dim(down_proj, index, 0, keepdims=False)
        produced = expert_apply(normed[picked], weight_both, weight_down)
        factor = jnp.where(valid, weight_row[picked], jnp.zeros_like(weight_row[picked]))
        contrib = produced.astype(jnp.float32) * factor[:, None]
        return (carry.at[picked].add(contrib), None)
    mixture, unused = lax.scan(per_expert, jnp.zeros((ROWS, D), jnp.float32), jnp.arange(EXPERTS, dtype=jnp.int32))
    return (hidden_state.astype(jnp.float32) + mixture).astype(jnp.bfloat16)
```

```python
import functools
import math

import jax
import jax.numpy as jnp
from jax import lax
from jax.experimental import pallas as pl
from jax.experimental.pallas import tpu as pltpu
from jax.sharding import PartitionSpec as P

MESH = pl.DeviceIdType.MESH
F32 = jnp.float32
BF16 = jnp.bfloat16
LANES = 128


def rotations(count, act):
    if count <= 17:
        for off in range(1, count):
            act(off)
    else:
        lax.fori_loop(1, count, lambda off, unused: (act(off), 0)[1], 0)


def kernel(
    dims,
    q_ref,
    res_ref,
    gain_ref,
    lists_ref,
    gates_ref,
    keys_hbm,
    values_hbm,
    ow_hbm,
    gu_hbm,
    dp_hbm,
    out_ref,
    keys,
    values,
    ow,
    gu,
    dp,
    qq,
    z,
    send1,
    recv1,
    ssend,
    srecv,
    wt,
    att,
    send2,
    recv2,
    send3,
    recv3,
    send4,
    recv4,
    send5,
    recv5,
    gmat,
    inner,
    load_sem,
    ssem1,
    rsem1,
    tsem1,
    usem1,
    ssem2,
    rsem2,
    ssem3,
    rsem3,
    ssem4,
    rsem4,
    ssem5,
    rsem5,
):
    n_ctx, n_head, n_pair, kv, group = dims
    n_all = n_ctx * n_head * n_pair
    n1 = n_ctx * n_pair
    n3 = n_ctx * n_head
    rows_here, width = res_ref.shape
    ci = lax.axis_index("ctx")
    hi = lax.axis_index("head")
    pi = lax.axis_index("pair")
    me = (ci * n_head + hi) * n_pair + pi

    flat = keys.shape[0]
    chunk = min(1024, flat)
    n_chunk = flat // chunk
    loads = []
    for b in range(n_chunk):
        piece = pl.ds(b * chunk, chunk)
        loads.append(
            pltpu.make_async_copy(keys_hbm.at[piece], keys.at[piece], load_sem.at[b])
        )
    vload = pltpu.make_async_copy(values_hbm, values, load_sem.at[n_chunk])
    oload = pltpu.make_async_copy(ow_hbm, ow, load_sem.at[n_chunk + 1])
    gload = pltpu.make_async_copy(gu_hbm.at[0], gu, load_sem.at[n_chunk + 2])
    dload = pltpu.make_async_copy(dp_hbm.at[0], dp, load_sem.at[n_chunk + 3])
    for load in loads + [vload, oload, gload, dload]:
        load.start()

    barrier = pltpu.get_barrier_semaphore()

    def coords(f):
        return {"ctx": f // (n_head * n_pair), "head": (f // n_pair) % n_head, "pair": f % n_pair}

    def greet(off):
        pl.semaphore_signal(
            barrier, inc=1, device_id=coords((me + off) % n_all), device_id_type=MESH
        )

    rotations(n_all, greet)

    for k in range(kv):
        place = 0
        for c in range(n_ctx):
            for p in range(n_pair):
                rows = []
                for h in range(n_head):
                    for i in range(rows_here):
                        r = ((c * n_head + h) * n_pair + p) * rows_here + i
                        rows.append(q_ref[r].astype(F32)[k * group : (k + 1) * group])
                block = jnp.concatenate(rows, axis=0).astype(BF16)
                qq[place : place + block.shape[0], k * LANES : (k + 1) * LANES] = block
                place += block.shape[0]

    per_dest = n_head * rows_here * group
    q_all = n1 * per_dest
    qb = min(256, q_all)
    factor = math.log2(math.e) / math.sqrt(LANES)
    lane = lax.broadcasted_iota(jnp.int32, (qb, LANES), 1)

    def spread(piece):
        if kv == 1:
            return piece
        row = lax.broadcasted_iota(jnp.int32, piece.shape, 0) % kv
        return jnp.concatenate(
            [piece * (row == k).astype(F32).astype(BF16) for k in range(kv)], axis=1
        )

    def attend(b, first):
        rows = pl.ds(pl.multiple_of(b * qb, qb), qb)
        qs = qq[rows, :]
        top = None
        for t in range(n_chunk):
            if first:
                loads[t].wait()
            piece = spread(keys[t * chunk : (t + 1) * chunk, :])
            s = lax.dot_general(
                qs, piece, (((1,), (1,)), ((), ())), preferred_element_type=F32
            )
            z[:, t * chunk : (t + 1) * chunk] = s
            for l in range(chunk // LANES):
                part = s[:, l * LANES : (l + 1) * LANES]
                top = part if top is None else jnp.maximum(top, part)
        tops = [
            jnp.max(jnp.where(lane % kv == k, top, -jnp.inf), axis=1, keepdims=True)
            for k in range(kv)
        ]
        shift = jnp.broadcast_to(tops[0], (qb, LANES))
        for k in range(1, kv):
            shift = jnp.where(lane % kv == k, tops[k], shift)
        if first:
            vload.wait()
        numer = jnp.zeros((qb, kv * LANES), F32)
        total = jnp.zeros((qb, LANES), F32)
        for t in range(n_chunk):
            probs = []
            for l in range(chunk // LANES):
                at = t * chunk + l * LANES
                pr = jnp.exp2((z[:, at : at + LANES] - shift) * factor)
                total = total + pr
                probs.append(pr.astype(BF16))
            numer = numer + jnp.dot(
                jnp.concatenate(probs, axis=1),
                spread(values[t * chunk : (t + 1) * chunk, :]),
                preferred_element_type=F32,
            )
        stats = jnp.zeros((qb, LANES), F32)
        for k in range(kv):
            sums = jnp.sum(jnp.where(lane % kv == k, total, 0.0), axis=1, keepdims=True)
            stats = jnp.where(lane == k, tops[k], stats)
            stats = jnp.where(lane == kv + k, sums, stats)
        turned = jnp.transpose(stats)
        for x in range(qb // LANES):
            ssend[b * (qb // LANES) + x] = turned[:8, x * LANES : (x + 1) * LANES]
        for x in range(qb // per_dest):
            send1[b * (qb // per_dest) + x] = numer[
                x * per_dest : (x + 1) * per_dest
            ].astype(BF16)

    attend(0, True)
    if q_all > qb:
        lax.fori_loop(1, q_all // qb, lambda b, unused: (attend(b, False), 0)[1], 0)

    pl.semaphore_wait(barrier, n_all - 1)

    j = ci * n_pair + pi

    def copies1(off):
        d = (j + off) % n1
        device = {"ctx": d // n_pair, "pair": d % n_pair}
        return (
            pltpu.make_async_remote_copy(
                src_ref=ssend.at[d * per_dest // LANES],
                dst_ref=srecv.at[j],
                send_sem=tsem1.at[off],
                recv_sem=usem1.at[off],
                device_id=device,
                device_id_type=MESH,
            ),
            pltpu.make_async_remote_copy(
                src_ref=send1.at[d],
                dst_ref=recv1.at[j],
                send_sem=ssem1.at[off],
                recv_sem=rsem1.at[off],
                device_id=device,
                device_id_type=MESH,
            ),
        )

    def start_all(copies):
        return lambda off: [c.start() for c in copies(off)]

    def recv_all(copies):
        return lambda off: [c.wait_recv() for c in copies(off)]

    def sent_all(copies):
        return lambda off: [c.wait_send() for c in copies(off)]

    rotations(n1, start_all(copies1))
    srecv[j] = ssend[j * per_dest // LANES]
    recv1[j] = send1[j]

    block_rows, top_k = lists_ref.shape
    ids = lists_ref[...]
    gw = gates_ref[...]
    experts = lax.broadcasted_iota(jnp.int32, (block_rows, LANES), 1)
    table = jnp.zeros((block_rows, LANES), F32)
    for k in range(top_k):
        table = table + jnp.where(ids[:, k : k + 1] == experts, gw[:, k : k + 1], 0.0)
    gmat[...] = table

    rotations(n1, recv_all(copies1))
    offset = pl.multiple_of((j * per_dest) % LANES, 8)
    for k in range(kv):
        m = srecv[:, k, :]
        t = srecv[:, kv + k, :]
        e = jnp.exp2((m - jnp.max(m, axis=0, keepdims=True)) * factor)
        w = e / jnp.sum(e * t, axis=0, keepdims=True)
        wt[k] = jnp.transpose(w)
        scale = wt[k, pl.ds(offset, per_dest), :]
        acc = jnp.zeros((per_dest, LANES), F32)
        for s in range(n1):
            acc = acc + scale[:, s : s + 1] * recv1[
                s, :, k * LANES : (k + 1) * LANES
            ].astype(F32)
        att[k] = acc

    n_rows = n_head * rows_here
    mine = jnp.concatenate(
        [
            att[k, pl.ds(g, n_rows, stride=group), :]
            for k in range(kv)
            for g in range(group)
        ],
        axis=1,
    ).astype(BF16)
    send2[...] = mine

    def copies2(off):
        return (
            pltpu.make_async_remote_copy(
                src_ref=send2,
                dst_ref=recv2.at[ci],
                send_sem=ssem2.at[off],
                recv_sem=rsem2.at[off],
                device_id={"ctx": (ci + off) % n_ctx},
                device_id_type=MESH,
            ),
        )

    rotations(n_ctx, start_all(copies2))
    recv2[ci] = mine
    oload.wait()
    rotations(n_ctx, recv_all(copies2))
    lhs = jnp.concatenate([recv2[c].astype(F32) for c in range(n_ctx)], axis=0).astype(BF16)
    part = jnp.dot(lhs, ow[...], preferred_element_type=F32)
    for f in range(n3):
        send3[f] = part[f * rows_here : (f + 1) * rows_here]

    u = ci * n_head + hi

    def copies3(off):
        f = (u + off) % n3
        return (
            pltpu.make_async_remote_copy(
                src_ref=send3.at[f],
                dst_ref=recv3.at[u],
                send_sem=ssem3.at[off],
                recv_sem=rsem3.at[off],
                device_id={"ctx": f // n_head, "head": f % n_head},
                device_id_type=MESH,
            ),
        )

    rotations(n3, start_all(copies3))
    recv3[u] = send3[u]
    rotations(n3, recv_all(copies3))
    columns = []
    for c in range(n_ctx):
        piece = recv3[c * n_head]
        for h in range(1, n_head):
            piece = piece + recv3[c * n_head + h]
        columns.append(piece)
    hidden = (res_ref[...].astype(F32) + jnp.concatenate(columns, axis=1)).astype(BF16)
    as_float = hidden.astype(F32)
    normed = (
        as_float
        * lax.rsqrt(jnp.mean(as_float * as_float, axis=1, keepdims=True) + 1e-06)
        * gain_ref[...]
    ).astype(BF16)
    send4[...] = normed

    def copies4(off):
        return (
            pltpu.make_async_remote_copy(
                src_ref=send4,
                dst_ref=recv4.at[me],
                send_sem=ssem4.at[off],
                recv_sem=rsem4.at[off],
                device_id=coords((me + off) % n_all),
                device_id_type=MESH,
            ),
        )

    rotations(n_all, start_all(copies4))
    recv4[me] = normed
    gload.wait()
    dload.wait()
    rotations(n_all, recv_all(copies4))
    x = jnp.concatenate([recv4[d].astype(F32) for d in range(n_all)], axis=0).astype(BF16)

    hidden_units = dp.shape[0]
    tile = 256

    def up(n, unused):
        gate = jnp.dot(
            x, gu[:, pl.ds(pl.multiple_of(n * tile, tile), tile)], preferred_element_type=F32
        )
        lift = jnp.dot(
            x,
            gu[:, pl.ds(pl.multiple_of(hidden_units + n * tile, tile), tile)],
            preferred_element_type=F32,
        )
        inner[:, pl.ds(pl.multiple_of(n * tile, tile), tile)] = (
            gate / (1.0 + jnp.exp(-gate)) * lift
        ).astype(BF16)
        return unused

    lax.fori_loop(0, hidden_units // tile, up, 0)
    wide = 512

    def down(n, unused):
        cols = pl.ds(pl.multiple_of(n * wide, wide), wide)
        got = jnp.dot(inner[...], dp[:, cols], preferred_element_type=F32)
        for d in range(n_all):
            send5[d, :, cols] = got[d * rows_here : (d + 1) * rows_here].astype(BF16)
        return unused

    lax.fori_loop(0, width // wide, down, 0)

    def copies5(off):
        d = (me + off) % n_all
        return (
            pltpu.make_async_remote_copy(
                src_ref=send5.at[d],
                dst_ref=recv5.at[me],
                send_sem=ssem5.at[off],
                recv_sem=rsem5.at[off],
                device_id=coords(d),
                device_id_type=MESH,
            ),
        )

    rotations(n_all, start_all(copies5))
    recv5[me] = send5[me]
    own = gmat[pl.ds((hi * n_pair + pi) * rows_here, rows_here), :]
    rotations(n_all, recv_all(copies5))
    mixture = as_float
    for e in range(n_all):
        mixture = mixture + own[:, e : e + 1] * recv5[e].astype(F32)
    out_ref[...] = mixture.astype(BF16)
    for count, copies in ((n1, copies1), (n_ctx, copies2), (n3, copies3), (n_all, copies4), (n_all, copies5)):
        rotations(count, sent_all(copies))


def body(
    queries,
    prompt_keys,
    prompt_values,
    residual,
    out_weight,
    norm_gain,
    expert_lists,
    gate_weights,
    gate_up,
    down_proj,
):
    n_ctx = lax.axis_size("ctx")
    n_head = lax.axis_size("head")
    n_pair = lax.axis_size("pair")
    n_all = n_ctx * n_head * n_pair
    n1 = n_ctx * n_pair
    n3 = n_ctx * n_head
    rows_all, heads_here, head_size = queries.shape
    length, kv, unused = prompt_keys.shape
    group = heads_here // kv
    rows_here, width = residual.shape
    hidden_units = down_proj.shape[1]
    assert gate_up.shape[0] == 1 and head_size == LANES
    per_dest = n_head * rows_here * group
    q_all = n1 * per_dest
    qb = min(256, q_all)
    flat = length * kv
    n_load = flat // min(1024, flat) + 4
    features, cols = out_weight.shape
    n_rows = n_head * rows_here
    vmem = pl.BlockSpec(memory_space=pltpu.VMEM)
    hbm = pl.BlockSpec(memory_space=pl.ANY)
    dma = pltpu.SemaphoreType.DMA
    return pl.pallas_call(
        functools.partial(kernel, (n_ctx, n_head, n_pair, kv, group)),
        out_shape=jax.ShapeDtypeStruct(residual.shape, BF16),
        in_specs=[vmem] * 5 + [hbm] * 5,
        out_specs=vmem,
        scratch_shapes=[
            pltpu.VMEM((flat, LANES), BF16),
            pltpu.VMEM((flat, LANES), BF16),
            pltpu.VMEM((features, cols), BF16),
            pltpu.VMEM(gate_up.shape[1:], BF16),
            pltpu.VMEM(down_proj.shape[1:], BF16),
            pltpu.VMEM((q_all, kv * LANES), BF16),
            pltpu.VMEM((qb, flat), F32),
            pltpu.VMEM((n1, per_dest, kv * LANES), BF16),
            pltpu.VMEM((n1, per_dest, kv * LANES), BF16),
            pltpu.VMEM((q_all // LANES, 8, LANES), F32),
            pltpu.VMEM((n1, 8, LANES), F32),
            pltpu.VMEM((kv, LANES, n1), F32),
            pltpu.VMEM((kv, per_dest, LANES), F32),
            pltpu.VMEM((n_rows, features), BF16),
            pltpu.VMEM((n_ctx, n_rows, features), BF16),
            pltpu.VMEM((n3, rows_here, cols), F32),
            pltpu.VMEM((n3, rows_here, cols), F32),
            pltpu.VMEM((rows_here, width), BF16),
            pltpu.VMEM((n_all, rows_here, width), BF16),
            pltpu.VMEM((n_all, rows_here, width), BF16),
            pltpu.VMEM((n_all, rows_here, width), BF16),
            pltpu.VMEM((expert_lists.shape[0], LANES), F32),
            pltpu.VMEM((n_all * rows_here, hidden_units), BF16),
            dma((n_load,)),
            dma((n1,)),
            dma((n1,)),
            dma((n1,)),
            dma((n1,)),
            dma((n_ctx,)),
            dma((n_ctx,)),
            dma((n3,)),
            dma((n3,)),
            dma((n_all,)),
            dma((n_all,)),
            dma((n_all,)),
            dma((n_all,)),
        ],
        compiler_params=pltpu.CompilerParams(
            collective_id=0, has_side_effects=True, vmem_limit_bytes=60 * 1024 * 1024
        ),
        name="decode_step",
    )(
        queries,
        residual,
        norm_gain.reshape(1, width),
        expert_lists,
        gate_weights,
        prompt_keys.reshape(flat, LANES),
        prompt_values.reshape(flat, LANES),
        out_weight,
        gate_up,
        down_proj,
    )


def solution(mesh):
    in_specs = (
        P("groups", "head", None),
        P(("groups", "ctx", "pair"), "head", None),
        P(("groups", "ctx", "pair"), "head", None),
        P(("groups", "ctx", "head", "pair"), None),
        P("head", "ctx"),
        P(),
        P(("groups", "ctx"), None),
        P(("groups", "ctx"), None),
        P(("ctx", "head", "pair"), None, None),
        P(("ctx", "head", "pair"), None, None),
    )
    out_specs = P(("groups", "ctx", "head", "pair"), None)
    return jax.shard_map(body, mesh=mesh, in_specs=in_specs, out_specs=out_specs, check_vma=False)
```

```python
import functools
import math

import jax
import jax.numpy as jnp
from jax import lax
from jax.experimental import pallas as pl
from jax.experimental.pallas import tpu as pltpu
from jax.sharding import PartitionSpec as P

MESH = pl.DeviceIdType.MESH
F32 = jnp.float32
BF16 = jnp.bfloat16
LANES = 128


def each(count, act):
    if count <= 17:
        for i in range(count):
            act(i)
    else:
        lax.fori_loop(0, count, lambda i, unused: (act(i), 0)[1], 0)


def far_first(at, count, step):
    down = count - 1 - step
    down = down - (at - down + count) // count
    up = step + (step - at + count) // count
    upper = at // ((count + 1) // 2)
    return down + upper * (up - down)


def kernel(
    dims,
    q_ref,
    res_ref,
    gain_ref,
    lists_ref,
    gates_ref,
    keys_hbm,
    values_hbm,
    ow_hbm,
    gu_hbm,
    dp_hbm,
    out_ref,
    keys,
    values,
    ow,
    gu,
    dp,
    qq,
    z,
    send1,
    recv1,
    ssend,
    srecv,
    wt,
    att,
    rres,
    send2,
    recv2,
    send3,
    recv3,
    send4,
    recv4,
    send5,
    recv5,
    gmat,
    inner,
    hid,
    load_sem,
    ssem1,
    rsem1,
    tsem1,
    usem1,
    ssem2,
    rsem2,
    ssem3,
    rsem3,
    ssem4,
    rsem4,
    ssem5,
    rsem5,
    ssem6,
    rsem6,
):
    n_ctx, n_head, n_pair, kv, group = dims
    n_all = n_ctx * n_head * n_pair
    n1 = n_ctx * n_pair
    rows_here, width = res_ref.shape
    ci = lax.axis_index("ctx")
    hi = lax.axis_index("head")
    pi = lax.axis_index("pair")
    me = (ci * n_head + hi) * n_pair + pi

    flat = keys.shape[0]
    chunk = min(1024, flat)
    n_chunk = flat // chunk
    loads = []
    for b in range(n_chunk):
        piece = pl.ds(b * chunk, chunk)
        loads.append(
            pltpu.make_async_copy(keys_hbm.at[piece], keys.at[piece], load_sem.at[b])
        )
    vload = pltpu.make_async_copy(values_hbm, values, load_sem.at[n_chunk])
    oload = pltpu.make_async_copy(ow_hbm, ow, load_sem.at[n_chunk + 1])
    gload = pltpu.make_async_copy(gu_hbm.at[0], gu, load_sem.at[n_chunk + 2])
    dload = pltpu.make_async_copy(dp_hbm.at[0], dp, load_sem.at[n_chunk + 3])
    for load in loads + [vload, oload, gload, dload]:
        load.start()

    barrier = pltpu.get_barrier_semaphore()
    nv = n_head * n_pair
    v_me = hi * n_pair + pi

    def everyone(act):
        def outside(i):
            act(far_first(ci, n_ctx, i // nv), (v_me + i) % nv)

        each((n_ctx - 1) * nv, outside)
        each(nv - 1, lambda i: act(ci, (v_me + 1 + i) % nv))

    def column(act):
        def outside(i):
            act(far_first(ci, n_ctx, i // n_pair), (pi + i) % n_pair)

        each((n_ctx - 1) * n_pair, outside)
        each(n_pair - 1, lambda i: act(ci, (pi + 1 + i) % n_pair))

    def line(act):
        each(n_ctx - 1, lambda i: act(far_first(ci, n_ctx, i)))

    def heads(act):
        each(n_head - 1, lambda i: act((hi + 1 + i) % n_head))

    def place(c, v):
        return {"ctx": c, "head": v // n_pair, "pair": v % n_pair}

    def remote(src, dst, sends, receives, to, slot, device):
        def made(place, semaphore):
            return pltpu.make_async_remote_copy(
                src_ref=src,
                dst_ref=dst.at[place],
                send_sem=sends.at[to],
                recv_sem=receives.at[semaphore],
                device_id=device,
                device_id_type=MESH,
            )

        return functools.partial(made, slot, slot), functools.partial(made, to, to)

    def greet(c, v):
        pl.semaphore_signal(barrier, inc=1, device_id=place(c, v), device_id_type=MESH)

    everyone(greet)

    for k in range(kv):
        filled = 0
        for c in range(n_ctx):
            for p in range(n_pair):
                rows = []
                for h in range(n_head):
                    for i in range(rows_here):
                        r = ((c * n_head + h) * n_pair + p) * rows_here + i
                        rows.append(q_ref[r].astype(F32)[k * group : (k + 1) * group])
                block = jnp.concatenate(rows, axis=0).astype(BF16)
                qq[filled : filled + block.shape[0], k * LANES : (k + 1) * LANES] = block
                filled += block.shape[0]

    per_dest = n_head * rows_here * group
    q_all = n1 * per_dest
    qb = min(256, q_all)
    factor = math.log2(math.e) / math.sqrt(LANES)
    lane = lax.broadcasted_iota(jnp.int32, (qb, LANES), 1)

    def spread(piece):
        if kv == 1:
            return piece
        row = lax.broadcasted_iota(jnp.int32, piece.shape, 0) % kv
        return jnp.concatenate(
            [piece * (row == k).astype(F32).astype(BF16) for k in range(kv)], axis=1
        )

    def attend(b, first):
        rows = pl.ds(pl.multiple_of(b * qb, qb), qb)
        qs = qq[rows, :]
        top = None
        for t in range(n_chunk):
            if first:
                loads[t].wait()
            piece = spread(keys[t * chunk : (t + 1) * chunk, :])
            s = lax.dot_general(
                qs, piece, (((1,), (1,)), ((), ())), preferred_element_type=F32
            )
            z[:, t * chunk : (t + 1) * chunk] = s
            for l in range(chunk // LANES):
                part = s[:, l * LANES : (l + 1) * LANES]
                top = part if top is None else jnp.maximum(top, part)
        if first:
            pl.semaphore_wait(barrier, n_all - 1)
            line(lambda c: copy6(c)[0]().start())
        tops = [
            jnp.max(jnp.where(lane % kv == k, top, -jnp.inf), axis=1, keepdims=True)
            for k in range(kv)
        ]
        shift = jnp.broadcast_to(tops[0], (qb, LANES))
        for k in range(1, kv):
            shift = jnp.where(lane % kv == k, tops[k], shift)
        if first:
            vload.wait()
        numer = jnp.zeros((qb, kv * LANES), F32)
        total = jnp.zeros((qb, LANES), F32)
        for t in range(n_chunk):
            probs = []
            for l in range(chunk // LANES):
                at = t * chunk + l * LANES
                pr = jnp.exp2((z[:, at : at + LANES] - shift) * factor)
                total = total + pr
                probs.append(pr.astype(BF16))
            numer = numer + jnp.dot(
                jnp.concatenate(probs, axis=1),
                spread(values[t * chunk : (t + 1) * chunk, :]),
                preferred_element_type=F32,
            )
        stats = jnp.zeros((qb, LANES), F32)
        for k in range(kv):
            sums = jnp.sum(jnp.where(lane % kv == k, total, 0.0), axis=1, keepdims=True)
            stats = jnp.where(lane == k, tops[k], stats)
            stats = jnp.where(lane == kv + k, sums, stats)
        turned = jnp.transpose(stats)
        for x in range(qb // LANES):
            ssend[b * (qb // LANES) + x] = turned[: 2 * kv, x * LANES : (x + 1) * LANES]
        for x in range(qb // per_dest):
            send1[b * (qb // per_dest) + x] = numer[
                x * per_dest : (x + 1) * per_dest
            ].astype(BF16)

    cols = ow.shape[1]

    def copy6(c):
        return remote(
            res_ref.at[:, pl.ds(pl.multiple_of(c * cols, LANES), cols)],
            rres, ssem6, rsem6, c, ci, {"ctx": c},
        )

    rres[ci] = res_ref[:, pl.ds(pl.multiple_of(ci * cols, LANES), cols)]
    attend(0, True)
    if q_all > qb:
        lax.fori_loop(1, q_all // qb, lambda b, unused: (attend(b, False), 0)[1], 0)

    j = ci * n_pair + pi

    def copies1(c, p):
        d = c * n_pair + p
        device = {"ctx": c, "pair": p}
        return (
            remote(ssend.at[d * per_dest // LANES], srecv, tsem1, usem1, d, j, device),
            remote(send1.at[d], recv1, ssem1, rsem1, d, j, device),
        )

    column(lambda c, p: [out().start() for out, back in copies1(c, p)])
    srecv[j] = ssend[j * per_dest // LANES]
    recv1[j] = send1[j]

    block_rows, top_k = lists_ref.shape
    ids = lists_ref[...]
    gw = gates_ref[...]
    experts = lax.broadcasted_iota(jnp.int32, (block_rows, LANES), 1)
    table = jnp.zeros((block_rows, LANES), F32)
    for k in range(top_k):
        table = table + jnp.where(ids[:, k : k + 1] == experts, gw[:, k : k + 1], 0.0)
    gmat[...] = table

    column(lambda c, p: [back().wait_recv() for out, back in copies1(c, p)])
    offset = pl.multiple_of((j * per_dest) % LANES, 8)
    for k in range(kv):
        m = srecv[:, k, :]
        t = srecv[:, kv + k, :]
        e = jnp.exp2((m - jnp.max(m, axis=0, keepdims=True)) * factor)
        w = e / jnp.sum(e * t, axis=0, keepdims=True)
        wt[k] = jnp.transpose(w)
        scale = wt[k, pl.ds(offset, per_dest), :]
        acc = jnp.zeros((per_dest, LANES), F32)
        for s in range(n1):
            acc = acc + scale[:, s : s + 1] * recv1[
                s, :, k * LANES : (k + 1) * LANES
            ].astype(F32)
        att[k] = acc

    n_rows = n_head * rows_here
    mine = jnp.concatenate(
        [
            att[k, pl.ds(g, n_rows, stride=group), :]
            for k in range(kv)
            for g in range(group)
        ],
        axis=1,
    ).astype(BF16)
    send2[...] = mine

    def copy2(c):
        return remote(send2, recv2, ssem2, rsem2, c, ci, {"ctx": c})

    line(lambda c: copy2(c)[0]().start())
    recv2[ci] = mine
    oload.wait()
    line(lambda c: copy2(c)[1]().wait_recv())
    arrived = [recv2[c].astype(F32) for c in range(n_ctx)]
    lhs = jnp.concatenate(
        [
            rows[h * rows_here : (h + 1) * rows_here]
            for h in range(n_head)
            for rows in arrived
        ],
        axis=0,
    ).astype(BF16)
    part = jnp.dot(lhs, ow[...], preferred_element_type=F32)
    n_sum = n_ctx * rows_here
    for h in range(n_head):
        send3[h] = part[h * n_sum : (h + 1) * n_sum]

    def copy3(h):
        return remote(send3.at[h], recv3, ssem3, rsem3, h, hi, {"head": h})

    heads(lambda h: copy3(h)[0]().start())
    recv3[hi] = send3[hi]
    line(lambda c: copy6(c)[1]().wait_recv())
    residual = jnp.concatenate([rres[c].astype(F32) for c in range(n_ctx)], axis=0)
    heads(lambda h: copy3(h)[1]().wait_recv())
    projected = recv3[0]
    for h in range(1, n_head):
        projected = projected + recv3[h]
    send4[...] = (residual + projected).astype(BF16)

    def copy4(c, v):
        return remote(send4, recv4, ssem4, rsem4, c * nv + v, me, place(c, v))

    everyone(lambda c, v: copy4(c, v)[0]().start())
    recv4[me] = send4[...]
    gload.wait()
    dload.wait()
    everyone(lambda c, v: copy4(c, v)[1]().wait_recv())
    normed = []
    for v in range(nv):
        hidden = jnp.concatenate(
            [recv4[c * nv + v].astype(F32) for c in range(n_ctx)], axis=1
        )
        for c in range(n_ctx):
            hid[v, c] = hidden[c * rows_here : (c + 1) * rows_here]
        square = jnp.mean(hidden * hidden, axis=1, keepdims=True)
        normed.append(hidden * lax.rsqrt(square + 1e-06) * gain_ref[...])
    x = jnp.concatenate(normed, axis=0).astype(BF16)

    hidden_units = dp.shape[0]
    tile = 256

    def up(n, unused):
        gate = jnp.dot(
            x, gu[:, pl.ds(pl.multiple_of(n * tile, tile), tile)], preferred_element_type=F32
        )
        lift = jnp.dot(
            x,
            gu[:, pl.ds(pl.multiple_of(hidden_units + n * tile, tile), tile)],
            preferred_element_type=F32,
        )
        inner[:, pl.ds(pl.multiple_of(n * tile, tile), tile)] = (
            gate / (1.0 + jnp.exp(-gate)) * lift
        ).astype(BF16)
        return unused

    lax.fori_loop(0, hidden_units // tile, up, 0)

    parts = send5.shape[0]
    wide = width // parts

    def copy5(b, c, v):
        d = c * nv + v
        return remote(
            send5.at[b, d], recv5.at[b], ssem5.at[b], rsem5.at[b], d, me, place(c, v)
        )

    for b in range(parts):
        got = jnp.dot(
            inner[...], dp[:, b * wide : (b + 1) * wide], preferred_element_type=F32
        ).astype(BF16).astype(F32)
        for c in range(n_ctx):
            for v in range(nv):
                at = v * n_sum + c * rows_here
                send5[b, c * nv + v] = got[at : at + rows_here].astype(BF16)
        everyone(lambda c, v: copy5(b, c, v)[0]().start())
        recv5[b, me] = send5[b, me]
    own = gmat[pl.ds(v_me * rows_here, rows_here), :]
    mine = hid[v_me, ci]
    for b in range(parts):
        everyone(lambda c, v: copy5(b, c, v)[1]().wait_recv())
        mixture = mine[:, b * wide : (b + 1) * wide]
        for e in range(n_all):
            mixture = mixture + own[:, e : e + 1] * recv5[b, e].astype(F32)
        out_ref[:, b * wide : (b + 1) * wide] = mixture
    line(lambda c: copy6(c)[0]().wait_send())
    column(lambda c, p: [out().wait_send() for out, back in copies1(c, p)])
    line(lambda c: copy2(c)[0]().wait_send())
    heads(lambda h: copy3(h)[0]().wait_send())
    everyone(lambda c, v: copy4(c, v)[0]().wait_send())
    for b in range(parts):
        everyone(lambda c, v: copy5(b, c, v)[0]().wait_send())


def body(
    queries,
    prompt_keys,
    prompt_values,
    residual,
    out_weight,
    norm_gain,
    expert_lists,
    gate_weights,
    gate_up,
    down_proj,
):
    n_ctx = lax.axis_size("ctx")
    n_head = lax.axis_size("head")
    n_pair = lax.axis_size("pair")
    n_all = n_ctx * n_head * n_pair
    n1 = n_ctx * n_pair
    rows_all, heads_here, head_size = queries.shape
    length, kv, unused = prompt_keys.shape
    group = heads_here // kv
    rows_here, width = residual.shape
    hidden_units = down_proj.shape[1]
    assert gate_up.shape[0] == 1 and head_size == LANES
    per_dest = n_head * rows_here * group
    q_all = n1 * per_dest
    qb = min(256, q_all)
    flat = length * kv
    n_load = flat // min(1024, flat) + 4
    features, cols = out_weight.shape
    n_rows = n_head * rows_here
    n_sum = n_ctx * rows_here
    parts = 2
    vmem = pl.BlockSpec(memory_space=pltpu.VMEM)
    hbm = pl.BlockSpec(memory_space=pl.ANY)
    dma = pltpu.SemaphoreType.DMA
    return pl.pallas_call(
        functools.partial(kernel, (n_ctx, n_head, n_pair, kv, group)),
        out_shape=jax.ShapeDtypeStruct(residual.shape, F32),
        in_specs=[vmem] * 5 + [hbm] * 5,
        out_specs=vmem,
        scratch_shapes=[
            pltpu.VMEM((flat, LANES), BF16),
            pltpu.VMEM((flat, LANES), BF16),
            pltpu.VMEM((features, cols), BF16),
            pltpu.VMEM(gate_up.shape[1:], BF16),
            pltpu.VMEM(down_proj.shape[1:], BF16),
            pltpu.VMEM((q_all, kv * LANES), BF16),
            pltpu.VMEM((qb, flat), F32),
            pltpu.VMEM((n1, per_dest, kv * LANES), BF16),
            pltpu.VMEM((n1, per_dest, kv * LANES), BF16),
            pltpu.VMEM((q_all // LANES, 2 * kv, LANES), F32),
            pltpu.VMEM((n1, 2 * kv, LANES), F32),
            pltpu.VMEM((kv, LANES, n1), F32),
            pltpu.VMEM((kv, per_dest, LANES), F32),
            pltpu.VMEM((n_ctx, rows_here, cols), BF16),
            pltpu.VMEM((n_rows, features), BF16),
            pltpu.VMEM((n_ctx, n_rows, features), BF16),
            pltpu.VMEM((n_head, n_sum, cols), F32),
            pltpu.VMEM((n_head, n_sum, cols), F32),
            pltpu.VMEM((n_sum, cols), BF16),
            pltpu.VMEM((n_all, n_sum, cols), BF16),
            pltpu.VMEM((parts, n_all, rows_here, width // parts), BF16),
            pltpu.VMEM((parts, n_all, rows_here, width // parts), BF16),
            pltpu.VMEM((expert_lists.shape[0], LANES), F32),
            pltpu.VMEM((n_all * rows_here, hidden_units), BF16),
            pltpu.VMEM((n_head * n_pair, n_ctx, rows_here, width), F32),
            dma((n_load,)),
            dma((n1,)),
            dma((n1,)),
            dma((n1,)),
            dma((n1,)),
            dma((n_ctx,)),
            dma((n_ctx,)),
            dma((n_head,)),
            dma((n_head,)),
            dma((n_all,)),
            dma((n_all,)),
            dma((parts, n_all)),
            dma((parts, n_all)),
            dma((n_ctx,)),
            dma((n_ctx,)),
        ],
        compiler_params=pltpu.CompilerParams(
            collective_id=0, has_side_effects=True, vmem_limit_bytes=60 * 1024 * 1024
        ),
        name="decode_step",
    )(
        queries,
        residual,
        norm_gain.reshape(1, width),
        expert_lists,
        gate_weights,
        prompt_keys.reshape(flat, LANES),
        prompt_values.reshape(flat, LANES),
        out_weight,
        gate_up,
        down_proj,
    ).astype(BF16)


def solution(mesh):
    in_specs = (
        P("groups", "head", None),
        P(("groups", "ctx", "pair"), "head", None),
        P(("groups", "ctx", "pair"), "head", None),
        P(("groups", "ctx", "head", "pair"), None),
        P("head", "ctx"),
        P(),
        P(("groups", "ctx"), None),
        P(("groups", "ctx"), None),
        P(("ctx", "head", "pair"), None, None),
        P(("ctx", "head", "pair"), None, None),
    )
    out_specs = P(("groups", "ctx", "head", "pair"), None)
    return jax.shard_map(body, mesh=mesh, in_specs=in_specs, out_specs=out_specs, check_vma=False)
```

```python
import functools
import math

import jax
import jax.numpy as jnp
from jax import lax
from jax.experimental import pallas as pl
from jax.experimental.pallas import tpu as pltpu
from jax.sharding import PartitionSpec as P

MESH = pl.DeviceIdType.MESH
F32 = jnp.float32
BF16 = jnp.bfloat16
LANES = 128


def each(count, act):
    if count <= 17:
        for i in range(count):
            act(i)
    else:
        lax.fori_loop(0, count, lambda i, unused: (act(i), 0)[1], 0)


def far_first(at, count, step):
    down = count - 1 - step
    down = down - (at - down + count) // count
    up = step + (step - at + count) // count
    upper = at // ((count + 1) // 2)
    return down + upper * (up - down)


def kernel(
    dims,
    q_ref,
    res_ref,
    gain_ref,
    lists_ref,
    gates_ref,
    keys_hbm,
    values_hbm,
    ow_hbm,
    gu_hbm,
    dp_hbm,
    out_ref,
    keys,
    values,
    ow,
    gu,
    dp,
    qq,
    z,
    send1,
    recv1,
    ssend,
    srecv,
    wt,
    att,
    rres,
    send2,
    recv2,
    send3,
    recv3,
    send4,
    recv4,
    send5,
    recv5,
    gmat,
    inner,
    hid,
    load_sem,
    ssem1,
    rsem1,
    tsem1,
    usem1,
    ssem2,
    rsem2,
    ssem3,
    rsem3,
    ssem4,
    rsem4,
    ssem5,
    rsem5,
    ssem6,
    rsem6,
):
    n_ctx, n_head, n_pair, kv, group = dims
    n_all = n_ctx * n_head * n_pair
    n1 = n_ctx * n_pair
    rows_here, width = res_ref.shape
    ci = lax.axis_index("ctx")
    hi = lax.axis_index("head")
    pi = lax.axis_index("pair")
    me = (ci * n_head + hi) * n_pair + pi

    flat = keys.shape[0]
    chunk = min(1024, flat)
    n_chunk = flat // chunk
    loads = []
    for b in range(n_chunk):
        piece = pl.ds(b * chunk, chunk)
        loads.append(
            pltpu.make_async_copy(keys_hbm.at[piece], keys.at[piece], load_sem.at[b])
        )
    vload = pltpu.make_async_copy(values_hbm, values, load_sem.at[n_chunk])
    oload = pltpu.make_async_copy(ow_hbm, ow, load_sem.at[n_chunk + 1])
    gload = pltpu.make_async_copy(gu_hbm.at[0], gu, load_sem.at[n_chunk + 2])
    dload = pltpu.make_async_copy(dp_hbm.at[0], dp, load_sem.at[n_chunk + 3])
    for load in loads + [vload, oload, gload, dload]:
        load.start()

    barrier = pltpu.get_barrier_semaphore()
    nv = n_head * n_pair
    v_me = hi * n_pair + pi

    def everyone(act):
        def outside(i):
            act(far_first(ci, n_ctx, i // nv), (v_me + i) % nv)

        each((n_ctx - 1) * nv, outside)
        each(nv - 1, lambda i: act(ci, (v_me + 1 + i) % nv))

    def column(act):
        def outside(i):
            act(far_first(ci, n_ctx, i // n_pair), (pi + i) % n_pair)

        each((n_ctx - 1) * n_pair, outside)
        each(n_pair - 1, lambda i: act(ci, (pi + 1 + i) % n_pair))

    def line(act):
        each(n_ctx - 1, lambda i: act(far_first(ci, n_ctx, i)))

    def heads(act):
        each(n_head - 1, lambda i: act((hi + 1 + i) % n_head))

    def place(c, v):
        return {"ctx": c, "head": v // n_pair, "pair": v % n_pair}

    def remote(src, dst, sends, receives, to, slot, device):
        def made(place, semaphore):
            return pltpu.make_async_remote_copy(
                src_ref=src,
                dst_ref=dst.at[place],
                send_sem=sends.at[to],
                recv_sem=receives.at[semaphore],
                device_id=device,
                device_id_type=MESH,
            )

        return functools.partial(made, slot, slot), functools.partial(made, to, to)

    def greet(c, v):
        pl.semaphore_signal(barrier, inc=1, device_id=place(c, v), device_id_type=MESH)

    everyone(greet)

    for k in range(kv):
        filled = 0
        for c in range(n_ctx):
            for p in range(n_pair):
                rows = []
                for h in range(n_head):
                    for i in range(rows_here):
                        r = ((c * n_head + h) * n_pair + p) * rows_here + i
                        rows.append(q_ref[r].astype(F32)[k * group : (k + 1) * group])
                block = jnp.concatenate(rows, axis=0).astype(BF16)
                qq[filled : filled + block.shape[0], k * LANES : (k + 1) * LANES] = block
                filled += block.shape[0]

    per_dest = n_head * rows_here * group
    q_all = n1 * per_dest
    qb = min(256, q_all)
    factor = math.log2(math.e) / math.sqrt(LANES)
    lane = lax.broadcasted_iota(jnp.int32, (qb, LANES), 1)

    def spread(piece):
        if kv == 1:
            return piece
        row = lax.broadcasted_iota(jnp.int32, piece.shape, 0) % kv
        return jnp.concatenate(
            [piece * (row == k).astype(F32).astype(BF16) for k in range(kv)], axis=1
        )

    def attend(b, first):
        rows = pl.ds(pl.multiple_of(b * qb, qb), qb)
        qs = qq[rows, :]
        top = None
        for t in range(n_chunk):
            if first:
                loads[t].wait()
            piece = spread(keys[t * chunk : (t + 1) * chunk, :])
            s = lax.dot_general(
                qs, piece, (((1,), (1,)), ((), ())), preferred_element_type=F32
            )
            z[:, t * chunk : (t + 1) * chunk] = s
            for l in range(chunk // LANES):
                part = s[:, l * LANES : (l + 1) * LANES]
                top = part if top is None else jnp.maximum(top, part)
        tops = [
            jnp.max(jnp.where(lane % kv == k, top, -jnp.inf), axis=1, keepdims=True)
            for k in range(kv)
        ]
        shift = jnp.broadcast_to(tops[0], (qb, LANES))
        for k in range(1, kv):
            shift = jnp.where(lane % kv == k, tops[k], shift)
        if first:
            vload.wait()
        numer = jnp.zeros((qb, kv * LANES), F32)
        total = jnp.zeros((qb, LANES), F32)
        for t in range(n_chunk):
            probs = []
            for l in range(chunk // LANES):
                at = t * chunk + l * LANES
                pr = jnp.exp2((z[:, at : at + LANES] - shift) * factor)
                total = total + pr
                probs.append(pr.astype(BF16))
            numer = numer + jnp.dot(
                jnp.concatenate(probs, axis=1),
                spread(values[t * chunk : (t + 1) * chunk, :]),
                preferred_element_type=F32,
            )
        stats = jnp.zeros((qb, LANES), F32)
        for k in range(kv):
            sums = jnp.sum(jnp.where(lane % kv == k, total, 0.0), axis=1, keepdims=True)
            stats = jnp.where(lane == k, tops[k], stats)
            stats = jnp.where(lane == kv + k, sums, stats)
        turned = jnp.transpose(stats)
        for x in range(qb // LANES):
            ssend[b * (qb // LANES) + x] = turned[: 2 * kv, x * LANES : (x + 1) * LANES]
        for x in range(qb // per_dest):
            send1[b * (qb // per_dest) + x] = numer[
                x * per_dest : (x + 1) * per_dest
            ].astype(BF16)

    cols = ow.shape[1]

    def copy6(c):
        return remote(
            res_ref.at[:, pl.ds(pl.multiple_of(c * cols, LANES), cols)],
            rres, ssem6, rsem6, c, ci, {"ctx": c},
        )

    rres[ci] = res_ref[:, pl.ds(pl.multiple_of(ci * cols, LANES), cols)]
    attend(0, True)
    if q_all > qb:
        lax.fori_loop(1, q_all // qb, lambda b, unused: (attend(b, False), 0)[1], 0)

    pl.semaphore_wait(barrier, n_all - 1)

    j = ci * n_pair + pi

    def copies1(c, p):
        d = c * n_pair + p
        device = {"ctx": c, "pair": p}
        return (
            remote(ssend.at[d * per_dest // LANES], srecv, tsem1, usem1, d, j, device),
            remote(send1.at[d], recv1, ssem1, rsem1, d, j, device),
        )

    column(lambda c, p: [out().start() for out, back in copies1(c, p)])
    line(lambda c: copy6(c)[0]().start())
    srecv[j] = ssend[j * per_dest // LANES]
    recv1[j] = send1[j]

    block_rows, top_k = lists_ref.shape
    ids = lists_ref[...]
    gw = gates_ref[...]
    experts = lax.broadcasted_iota(jnp.int32, (block_rows, LANES), 1)
    table = jnp.zeros((block_rows, LANES), F32)
    for k in range(top_k):
        table = table + jnp.where(ids[:, k : k + 1] == experts, gw[:, k : k + 1], 0.0)
    gmat[...] = table

    column(lambda c, p: [back().wait_recv() for out, back in copies1(c, p)])
    offset = pl.multiple_of((j * per_dest) % LANES, 8)
    for k in range(kv):
        m = srecv[:, k, :]
        t = srecv[:, kv + k, :]
        e = jnp.exp2((m - jnp.max(m, axis=0, keepdims=True)) * factor)
        w = e / jnp.sum(e * t, axis=0, keepdims=True)
        wt[k] = jnp.transpose(w)
        scale = wt[k, pl.ds(offset, per_dest), :]
        acc = jnp.zeros((per_dest, LANES), F32)
        for s in range(n1):
            acc = acc + scale[:, s : s + 1] * recv1[
                s, :, k * LANES : (k + 1) * LANES
            ].astype(F32)
        att[k] = acc

    n_rows = n_head * rows_here
    mine = jnp.concatenate(
        [
            att[k, pl.ds(g, n_rows, stride=group), :]
            for k in range(kv)
            for g in range(group)
        ],
        axis=1,
    ).astype(BF16)
    send2[...] = mine

    def copy2(c):
        return remote(send2, recv2, ssem2, rsem2, c, ci, {"ctx": c})

    line(lambda c: copy2(c)[0]().start())
    recv2[ci] = mine
    oload.wait()
    line(lambda c: copy2(c)[1]().wait_recv())
    arrived = [recv2[c].astype(F32) for c in range(n_ctx)]
    lhs = jnp.concatenate(
        [
            rows[h * rows_here : (h + 1) * rows_here]
            for h in range(n_head)
            for rows in arrived
        ],
        axis=0,
    ).astype(BF16)
    part = jnp.dot(lhs, ow[...], preferred_element_type=F32)
    n_sum = n_ctx * rows_here
    for h in range(n_head):
        send3[h] = part[h * n_sum : (h + 1) * n_sum]

    def copy3(h):
        return remote(send3.at[h], recv3, ssem3, rsem3, h, hi, {"head": h})

    heads(lambda h: copy3(h)[0]().start())
    recv3[hi] = send3[hi]
    line(lambda c: copy6(c)[1]().wait_recv())
    residual = jnp.concatenate([rres[c].astype(F32) for c in range(n_ctx)], axis=0)
    heads(lambda h: copy3(h)[1]().wait_recv())
    projected = recv3[0]
    for h in range(1, n_head):
        projected = projected + recv3[h]
    send4[...] = (residual + projected).astype(BF16)

    def copy4(c, v):
        return remote(send4, recv4, ssem4, rsem4, c * nv + v, me, place(c, v))

    everyone(lambda c, v: copy4(c, v)[0]().start())
    recv4[me] = send4[...]
    gload.wait()
    dload.wait()
    everyone(lambda c, v: copy4(c, v)[1]().wait_recv())
    normed = []
    for v in range(nv):
        hidden = jnp.concatenate(
            [recv4[c * nv + v].astype(F32) for c in range(n_ctx)], axis=1
        )
        for c in range(n_ctx):
            hid[v, c] = hidden[c * rows_here : (c + 1) * rows_here]
        square = jnp.mean(hidden * hidden, axis=1, keepdims=True)
        normed.append(hidden * lax.rsqrt(square + 1e-06) * gain_ref[...])
    x = jnp.concatenate(normed, axis=0).astype(BF16)

    hidden_units = dp.shape[0]
    tile = 256

    def up(n, unused):
        gate = jnp.dot(
            x, gu[:, pl.ds(pl.multiple_of(n * tile, tile), tile)], preferred_element_type=F32
        )
        lift = jnp.dot(
            x,
            gu[:, pl.ds(pl.multiple_of(hidden_units + n * tile, tile), tile)],
            preferred_element_type=F32,
        )
        inner[:, pl.ds(pl.multiple_of(n * tile, tile), tile)] = (
            gate / (1.0 + jnp.exp(-gate)) * lift
        ).astype(BF16)
        return unused

    lax.fori_loop(0, hidden_units // tile, up, 0)

    parts = send5.shape[0]
    wide = width // parts

    def copy5(b, c, v):
        d = c * nv + v
        return remote(
            send5.at[b, d], recv5.at[b], ssem5.at[b], rsem5.at[b], d, me, place(c, v)
        )

    for b in range(parts):
        got = jnp.dot(
            inner[...], dp[:, b * wide : (b + 1) * wide], preferred_element_type=F32
        ).astype(BF16).astype(F32)
        for c in range(n_ctx):
            for v in range(nv):
                at = v * n_sum + c * rows_here
                send5[b, c * nv + v] = got[at : at + rows_here].astype(BF16)
        everyone(lambda c, v: copy5(b, c, v)[0]().start())
        recv5[b, me] = send5[b, me]
    own = gmat[pl.ds(v_me * rows_here, rows_here), :]
    mine = hid[v_me, ci]
    for b in range(parts):
        everyone(lambda c, v: copy5(b, c, v)[1]().wait_recv())
        mixture = mine[:, b * wide : (b + 1) * wide]
        for e in range(n_all):
            mixture = mixture + own[:, e : e + 1] * recv5[b, e].astype(F32)
        out_ref[:, b * wide : (b + 1) * wide] = mixture
    line(lambda c: copy6(c)[0]().wait_send())
    column(lambda c, p: [out().wait_send() for out, back in copies1(c, p)])
    line(lambda c: copy2(c)[0]().wait_send())
    heads(lambda h: copy3(h)[0]().wait_send())
    everyone(lambda c, v: copy4(c, v)[0]().wait_send())
    for b in range(parts):
        everyone(lambda c, v: copy5(b, c, v)[0]().wait_send())


def body(
    queries,
    prompt_keys,
    prompt_values,
    residual,
    out_weight,
    norm_gain,
    expert_lists,
    gate_weights,
    gate_up,
    down_proj,
):
    n_ctx = lax.axis_size("ctx")
    n_head = lax.axis_size("head")
    n_pair = lax.axis_size("pair")
    n_all = n_ctx * n_head * n_pair
    n1 = n_ctx * n_pair
    rows_all, heads_here, head_size = queries.shape
    length, kv, unused = prompt_keys.shape
    group = heads_here // kv
    rows_here, width = residual.shape
    hidden_units = down_proj.shape[1]
    assert gate_up.shape[0] == 1 and head_size == LANES
    per_dest = n_head * rows_here * group
    q_all = n1 * per_dest
    qb = min(256, q_all)
    flat = length * kv
    n_load = flat // min(1024, flat) + 4
    features, cols = out_weight.shape
    n_rows = n_head * rows_here
    n_sum = n_ctx * rows_here
    parts = 2
    vmem = pl.BlockSpec(memory_space=pltpu.VMEM)
    hbm = pl.BlockSpec(memory_space=pl.ANY)
    dma = pltpu.SemaphoreType.DMA
    return pl.pallas_call(
        functools.partial(kernel, (n_ctx, n_head, n_pair, kv, group)),
        out_shape=jax.ShapeDtypeStruct(residual.shape, F32),
        in_specs=[vmem] * 5 + [hbm] * 5,
        out_specs=vmem,
        scratch_shapes=[
            pltpu.VMEM((flat, LANES), BF16),
            pltpu.VMEM((flat, LANES), BF16),
            pltpu.VMEM((features, cols), BF16),
            pltpu.VMEM(gate_up.shape[1:], BF16),
            pltpu.VMEM(down_proj.shape[1:], BF16),
            pltpu.VMEM((q_all, kv * LANES), BF16),
            pltpu.VMEM((qb, flat), F32),
            pltpu.VMEM((n1, per_dest, kv * LANES), BF16),
            pltpu.VMEM((n1, per_dest, kv * LANES), BF16),
            pltpu.VMEM((q_all // LANES, 2 * kv, LANES), F32),
            pltpu.VMEM((n1, 2 * kv, LANES), F32),
            pltpu.VMEM((kv, LANES, n1), F32),
            pltpu.VMEM((kv, per_dest, LANES), F32),
            pltpu.VMEM((n_ctx, rows_here, cols), BF16),
            pltpu.VMEM((n_rows, features), BF16),
            pltpu.VMEM((n_ctx, n_rows, features), BF16),
            pltpu.VMEM((n_head, n_sum, cols), F32),
            pltpu.VMEM((n_head, n_sum, cols), F32),
            pltpu.VMEM((n_sum, cols), BF16),
            pltpu.VMEM((n_all, n_sum, cols), BF16),
            pltpu.VMEM((parts, n_all, rows_here, width // parts), BF16),
            pltpu.VMEM((parts, n_all, rows_here, width // parts), BF16),
            pltpu.VMEM((expert_lists.shape[0], LANES), F32),
            pltpu.VMEM((n_all * rows_here, hidden_units), BF16),
            pltpu.VMEM((n_head * n_pair, n_ctx, rows_here, width), F32),
            dma((n_load,)),
            dma((n1,)),
            dma((n1,)),
            dma((n1,)),
            dma((n1,)),
            dma((n_ctx,)),
            dma((n_ctx,)),
            dma((n_head,)),
            dma((n_head,)),
            dma((n_all,)),
            dma((n_all,)),
            dma((parts, n_all)),
            dma((parts, n_all)),
            dma((n_ctx,)),
            dma((n_ctx,)),
        ],
        compiler_params=pltpu.CompilerParams(
            collective_id=0, has_side_effects=True, vmem_limit_bytes=60 * 1024 * 1024
        ),
        name="decode_step",
    )(
        queries,
        residual,
        norm_gain.reshape(1, width),
        expert_lists,
        gate_weights,
        prompt_keys.reshape(flat, LANES),
        prompt_values.reshape(flat, LANES),
        out_weight,
        gate_up,
        down_proj,
    ).astype(BF16)


def solution(mesh):
    in_specs = (
        P("groups", "head", None),
        P(("groups", "ctx", "pair"), "head", None),
        P(("groups", "ctx", "pair"), "head", None),
        P(("groups", "ctx", "head", "pair"), None),
        P("head", "ctx"),
        P(),
        P(("groups", "ctx"), None),
        P(("groups", "ctx"), None),
        P(("ctx", "head", "pair"), None, None),
        P(("ctx", "head", "pair"), None, None),
    )
    out_specs = P(("groups", "ctx", "head", "pair"), None)
    return jax.shard_map(body, mesh=mesh, in_specs=in_specs, out_specs=out_specs, check_vma=False)
```

```python
import functools
import math

import jax
import jax.numpy as jnp
from jax import lax
from jax.experimental import pallas as pl
from jax.experimental.pallas import tpu as pltpu
from jax.sharding import PartitionSpec as P

MESH = pl.DeviceIdType.MESH
F32 = jnp.float32
BF16 = jnp.bfloat16
LANES = 128


def each(count, act):
    if count <= 17:
        for i in range(count):
            act(i)
    else:
        lax.fori_loop(0, count, lambda i, unused: (act(i), 0)[1], 0)


def far_first(at, count, step):
    down = count - 1 - step
    down = down - (at - down + count) // count
    up = step + (step - at + count) // count
    upper = at // ((count + 1) // 2)
    return down + upper * (up - down)


def kernel(
    dims,
    q_hbm,
    res_hbm,
    gain_hbm,
    lists_hbm,
    gates_hbm,
    keys_hbm,
    values_hbm,
    ow_hbm,
    gu_hbm,
    dp_hbm,
    out_ref,
    q_ref,
    res_ref,
    gain_ref,
    lists_ref,
    gates_ref,
    keys,
    values,
    ow,
    gu,
    dp,
    qq,
    z,
    send1,
    recv1,
    ssend,
    srecv,
    wt,
    att,
    rres,
    send2,
    recv2,
    send3,
    recv3,
    send4,
    recv4,
    send5,
    recv5,
    gmat,
    inner,
    hid,
    load_sem,
    ssem1,
    rsem1,
    tsem1,
    usem1,
    ssem2,
    rsem2,
    ssem3,
    rsem3,
    ssem4,
    rsem4,
    ssem5,
    rsem5,
    ssem6,
    rsem6,
):
    n_ctx, n_head, n_pair, kv, group = dims
    n_all = n_ctx * n_head * n_pair
    n1 = n_ctx * n_pair
    rows_here, width = res_hbm.shape
    ci = lax.axis_index("ctx")
    hi = lax.axis_index("head")
    pi = lax.axis_index("pair")
    me = (ci * n_head + hi) * n_pair + pi

    flat = keys.shape[0]
    chunk = min(1024, flat)
    n_chunk = flat // chunk
    loads = []
    for b in range(n_chunk):
        piece = pl.ds(b * chunk, chunk)
        loads.append(
            pltpu.make_async_copy(keys_hbm.at[piece], keys.at[piece], load_sem.at[b])
        )
    vload = pltpu.make_async_copy(values_hbm, values, load_sem.at[n_chunk])
    oload = pltpu.make_async_copy(ow_hbm, ow, load_sem.at[n_chunk + 1])
    gload = pltpu.make_async_copy(gu_hbm.at[0], gu, load_sem.at[n_chunk + 2])
    dload = pltpu.make_async_copy(dp_hbm.at[0], dp, load_sem.at[n_chunk + 3])
    small = [
        pltpu.make_async_copy(src, dst, load_sem.at[n_chunk + 4 + i])
        for i, (src, dst) in enumerate(
            (
                (q_hbm, q_ref),
                (res_hbm, res_ref),
                (gain_hbm, gain_ref),
                (lists_hbm, lists_ref),
                (gates_hbm, gates_ref),
            )
        )
    ]
    for load in small[:1] + loads + [vload] + small[1:]:
        load.start()

    barrier = pltpu.get_barrier_semaphore()
    nv = n_head * n_pair
    v_me = hi * n_pair + pi

    def everyone(act):
        def outside(i):
            act(far_first(ci, n_ctx, i // nv), (v_me + i) % nv)

        each((n_ctx - 1) * nv, outside)
        each(nv - 1, lambda i: act(ci, (v_me + 1 + i) % nv))

    def column(act):
        def outside(i):
            act(far_first(ci, n_ctx, i // n_pair), (pi + i) % n_pair)

        each((n_ctx - 1) * n_pair, outside)
        each(n_pair - 1, lambda i: act(ci, (pi + 1 + i) % n_pair))

    def line(act):
        each(n_ctx - 1, lambda i: act(far_first(ci, n_ctx, i)))

    def heads(act):
        each(n_head - 1, lambda i: act((hi + 1 + i) % n_head))

    def place(c, v):
        return {"ctx": c, "head": v // n_pair, "pair": v % n_pair}

    def remote(src, dst, sends, receives, to, slot, device):
        def made(place, semaphore):
            return pltpu.make_async_remote_copy(
                src_ref=src,
                dst_ref=dst.at[place],
                send_sem=sends.at[to],
                recv_sem=receives.at[semaphore],
                device_id=device,
                device_id_type=MESH,
            )

        return functools.partial(made, slot, slot), functools.partial(made, to, to)

    def greet(c, v):
        pl.semaphore_signal(barrier, inc=1, device_id=place(c, v), device_id_type=MESH)

    everyone(greet)

    small[0].wait()
    for k in range(kv):
        filled = 0
        for c in range(n_ctx):
            for p in range(n_pair):
                rows = []
                for h in range(n_head):
                    for i in range(rows_here):
                        r = ((c * n_head + h) * n_pair + p) * rows_here + i
                        rows.append(q_ref[r].astype(F32)[k * group : (k + 1) * group])
                block = jnp.concatenate(rows, axis=0).astype(BF16)
                qq[filled : filled + block.shape[0], k * LANES : (k + 1) * LANES] = block
                filled += block.shape[0]

    per_dest = n_head * rows_here * group
    q_all = n1 * per_dest
    qb = min(256, q_all)
    factor = math.log2(math.e) / math.sqrt(LANES)
    lane = lax.broadcasted_iota(jnp.int32, (qb, LANES), 1)

    row = lax.broadcasted_iota(jnp.int32, (16, LANES), 0) % kv
    masks = [
        jnp.concatenate([(row == k).astype(F32).astype(BF16)] * (chunk // 16), axis=0)
        for k in range(kv)
    ]

    def spread(piece):
        if kv == 1:
            return piece
        return jnp.concatenate([piece * masks[k] for k in range(kv)], axis=1)

    def attend(b, first):
        rows = pl.ds(pl.multiple_of(b * qb, qb), qb)
        qs = qq[rows, :]
        top = None
        for t in range(n_chunk):
            if first:
                loads[t].wait()
            piece = spread(keys[t * chunk : (t + 1) * chunk, :])
            s = lax.dot_general(
                qs, piece, (((1,), (1,)), ((), ())), preferred_element_type=F32
            )
            z[:, t * chunk : (t + 1) * chunk] = s
            for l in range(chunk // LANES):
                part = s[:, l * LANES : (l + 1) * LANES]
                top = part if top is None else jnp.maximum(top, part)
        tops = [
            jnp.max(jnp.where(lane % kv == k, top, -jnp.inf), axis=1, keepdims=True)
            for k in range(kv)
        ]
        shift = jnp.broadcast_to(tops[0], (qb, LANES))
        for k in range(1, kv):
            shift = jnp.where(lane % kv == k, tops[k], shift)
        if first:
            vload.wait()
            for load in (oload, gload, dload):
                load.start()
        numer = jnp.zeros((qb, kv * LANES), F32)
        total = jnp.zeros((qb, LANES), F32)
        for t in range(n_chunk):
            probs = []
            for l in range(chunk // LANES):
                at = t * chunk + l * LANES
                pr = jnp.exp2((z[:, at : at + LANES] - shift) * factor)
                total = total + pr
                probs.append(pr.astype(BF16))
            numer = numer + jnp.dot(
                jnp.concatenate(probs, axis=1),
                spread(values[t * chunk : (t + 1) * chunk, :]),
                preferred_element_type=F32,
            )
        stats = jnp.zeros((qb, LANES), F32)
        for k in range(kv):
            sums = jnp.sum(jnp.where(lane % kv == k, total, 0.0), axis=1, keepdims=True)
            stats = jnp.where(lane == k, tops[k], stats)
            stats = jnp.where(lane == kv + k, sums, stats)
        turned = jnp.transpose(stats)
        for x in range(qb // LANES):
            ssend[b * (qb // LANES) + x] = turned[: 2 * kv, x * LANES : (x + 1) * LANES]
        for x in range(qb // per_dest):
            send1[b * (qb // per_dest) + x] = numer[
                x * per_dest : (x + 1) * per_dest
            ].astype(BF16)

    for load in small[1:]:
        load.wait()
    cols = ow.shape[1]

    def copy6(c):
        return remote(
            res_ref.at[:, pl.ds(pl.multiple_of(c * cols, LANES), cols)],
            rres, ssem6, rsem6, c, ci, {"ctx": c},
        )

    rres[ci] = res_ref[:, pl.ds(pl.multiple_of(ci * cols, LANES), cols)]
    attend(0, True)
    if q_all > qb:
        lax.fori_loop(1, q_all // qb, lambda b, unused: (attend(b, False), 0)[1], 0)

    pl.semaphore_wait(barrier, n_all - 1)

    j = ci * n_pair + pi

    def copies1(c, p):
        d = c * n_pair + p
        device = {"ctx": c, "pair": p}
        return (
            remote(ssend.at[d * per_dest // LANES], srecv, tsem1, usem1, d, j, device),
            remote(send1.at[d], recv1, ssem1, rsem1, d, j, device),
        )

    column(lambda c, p: [out().start() for out, back in copies1(c, p)])
    line(lambda c: copy6(c)[0]().start())
    srecv[j] = ssend[j * per_dest // LANES]
    recv1[j] = send1[j]

    block_rows, top_k = lists_ref.shape
    ids = lists_ref[...]
    gw = gates_ref[...]
    experts = lax.broadcasted_iota(jnp.int32, (block_rows, LANES), 1)
    table = jnp.zeros((block_rows, LANES), F32)
    for k in range(top_k):
        table = table + jnp.where(ids[:, k : k + 1] == experts, gw[:, k : k + 1], 0.0)
    gmat[...] = table

    column(lambda c, p: [back().wait_recv() for out, back in copies1(c, p)])
    offset = pl.multiple_of((j * per_dest) % LANES, 8)
    for k in range(kv):
        m = srecv[:, k, :]
        t = srecv[:, kv + k, :]
        e = jnp.exp2((m - jnp.max(m, axis=0, keepdims=True)) * factor)
        w = e / jnp.sum(e * t, axis=0, keepdims=True)
        wt[k] = jnp.transpose(w)
        scale = wt[k, pl.ds(offset, per_dest), :]
        acc = jnp.zeros((per_dest, LANES), F32)
        for s in range(n1):
            acc = acc + scale[:, s : s + 1] * recv1[
                s, :, k * LANES : (k + 1) * LANES
            ].astype(F32)
        att[k] = acc

    n_rows = n_head * rows_here
    mine = jnp.concatenate(
        [
            att[k, pl.ds(g, n_rows, stride=group), :]
            for k in range(kv)
            for g in range(group)
        ],
        axis=1,
    ).astype(BF16)
    send2[...] = mine

    def copy2(c):
        return remote(send2, recv2, ssem2, rsem2, c, ci, {"ctx": c})

    line(lambda c: copy2(c)[0]().start())
    recv2[ci] = mine
    oload.wait()
    line(lambda c: copy2(c)[1]().wait_recv())
    arrived = [recv2[c].astype(F32) for c in range(n_ctx)]
    lhs = jnp.concatenate(
        [
            rows[h * rows_here : (h + 1) * rows_here]
            for h in range(n_head)
            for rows in arrived
        ],
        axis=0,
    ).astype(BF16)
    part = jnp.dot(lhs, ow[...], preferred_element_type=F32)
    n_sum = n_ctx * rows_here
    for h in range(n_head):
        send3[h] = part[h * n_sum : (h + 1) * n_sum]

    def copy3(h):
        return remote(send3.at[h], recv3, ssem3, rsem3, h, hi, {"head": h})

    heads(lambda h: copy3(h)[0]().start())
    recv3[hi] = send3[hi]
    line(lambda c: copy6(c)[1]().wait_recv())
    residual = jnp.concatenate([rres[c].astype(F32) for c in range(n_ctx)], axis=0)
    heads(lambda h: copy3(h)[1]().wait_recv())
    projected = recv3[0]
    for h in range(1, n_head):
        projected = projected + recv3[h]
    send4[...] = (residual + projected).astype(BF16)

    def copy4(c, v):
        return remote(send4, recv4, ssem4, rsem4, c * nv + v, me, place(c, v))

    everyone(lambda c, v: copy4(c, v)[0]().start())
    recv4[me] = send4[...]
    gload.wait()
    dload.wait()
    everyone(lambda c, v: copy4(c, v)[1]().wait_recv())
    normed = []
    for v in range(nv):
        hidden = jnp.concatenate(
            [recv4[c * nv + v].astype(F32) for c in range(n_ctx)], axis=1
        )
        for c in range(n_ctx):
            hid[v, c] = hidden[c * rows_here : (c + 1) * rows_here]
        square = jnp.mean(hidden * hidden, axis=1, keepdims=True)
        normed.append(hidden * lax.rsqrt(square + 1e-06) * gain_ref[...])
    x = jnp.concatenate(normed, axis=0).astype(BF16)

    hidden_units = dp.shape[0]
    tile = 256

    def up(n, unused):
        gate = jnp.dot(
            x, gu[:, pl.ds(pl.multiple_of(n * tile, tile), tile)], preferred_element_type=F32
        )
        lift = jnp.dot(
            x,
            gu[:, pl.ds(pl.multiple_of(hidden_units + n * tile, tile), tile)],
            preferred_element_type=F32,
        )
        inner[:, pl.ds(pl.multiple_of(n * tile, tile), tile)] = (
            gate / (1.0 + jnp.exp(-gate)) * lift
        ).astype(BF16)
        return unused

    lax.fori_loop(0, hidden_units // tile, up, 0)

    parts = send5.shape[0]
    wide = width // parts

    def copy5(b, c, v):
        d = c * nv + v
        return remote(
            send5.at[b, d], recv5.at[b], ssem5.at[b], rsem5.at[b], d, me, place(c, v)
        )

    for b in range(parts):
        got = jnp.dot(
            inner[...], dp[:, b * wide : (b + 1) * wide], preferred_element_type=F32
        ).astype(BF16).astype(F32)
        for c in range(n_ctx):
            for v in range(nv):
                at = v * n_sum + c * rows_here
                send5[b, c * nv + v] = got[at : at + rows_here].astype(BF16)
        everyone(lambda c, v: copy5(b, c, v)[0]().start())
        recv5[b, me] = send5[b, me]
    own = gmat[pl.ds(v_me * rows_here, rows_here), :]
    mine = hid[v_me, ci]
    for b in range(parts):
        everyone(lambda c, v: copy5(b, c, v)[1]().wait_recv())
        mixture = mine[:, b * wide : (b + 1) * wide]
        for e in range(n_all):
            mixture = mixture + own[:, e : e + 1] * recv5[b, e].astype(F32)
        out_ref[:, b * wide : (b + 1) * wide] = mixture
    line(lambda c: copy6(c)[0]().wait_send())
    column(lambda c, p: [out().wait_send() for out, back in copies1(c, p)])
    line(lambda c: copy2(c)[0]().wait_send())
    heads(lambda h: copy3(h)[0]().wait_send())
    everyone(lambda c, v: copy4(c, v)[0]().wait_send())
    for b in range(parts):
        everyone(lambda c, v: copy5(b, c, v)[0]().wait_send())


def body(
    queries,
    prompt_keys,
    prompt_values,
    residual,
    out_weight,
    norm_gain,
    expert_lists,
    gate_weights,
    gate_up,
    down_proj,
):
    n_ctx = lax.axis_size("ctx")
    n_head = lax.axis_size("head")
    n_pair = lax.axis_size("pair")
    n_all = n_ctx * n_head * n_pair
    n1 = n_ctx * n_pair
    rows_all, heads_here, head_size = queries.shape
    length, kv, unused = prompt_keys.shape
    group = heads_here // kv
    rows_here, width = residual.shape
    hidden_units = down_proj.shape[1]
    assert gate_up.shape[0] == 1 and head_size == LANES
    per_dest = n_head * rows_here * group
    q_all = n1 * per_dest
    qb = min(256, q_all)
    flat = length * kv
    n_load = flat // min(1024, flat) + 9
    features, cols = out_weight.shape
    n_rows = n_head * rows_here
    n_sum = n_ctx * rows_here
    parts = 2
    vmem = pl.BlockSpec(memory_space=pltpu.VMEM)
    hbm = pl.BlockSpec(memory_space=pltpu.HBM)
    dma = pltpu.SemaphoreType.DMA
    return pl.pallas_call(
        functools.partial(kernel, (n_ctx, n_head, n_pair, kv, group)),
        out_shape=jax.ShapeDtypeStruct(residual.shape, F32),
        in_specs=[hbm] * 10,
        out_specs=vmem,
        scratch_shapes=[
            pltpu.VMEM(queries.shape, BF16),
            pltpu.VMEM(residual.shape, BF16),
            pltpu.VMEM((1, width), F32),
            pltpu.VMEM(expert_lists.shape, jnp.int32),
            pltpu.VMEM(gate_weights.shape, F32),
            pltpu.VMEM((flat, LANES), BF16),
            pltpu.VMEM((flat, LANES), BF16),
            pltpu.VMEM((features, cols), BF16),
            pltpu.VMEM(gate_up.shape[1:], BF16),
            pltpu.VMEM(down_proj.shape[1:], BF16),
            pltpu.VMEM((q_all, kv * LANES), BF16),
            pltpu.VMEM((qb, flat), F32),
            pltpu.VMEM((n1, per_dest, kv * LANES), BF16),
            pltpu.VMEM((n1, per_dest, kv * LANES), BF16),
            pltpu.VMEM((q_all // LANES, 2 * kv, LANES), F32),
            pltpu.VMEM((n1, 2 * kv, LANES), F32),
            pltpu.VMEM((kv, LANES, n1), F32),
            pltpu.VMEM((kv, per_dest, LANES), F32),
            pltpu.VMEM((n_ctx, rows_here, cols), BF16),
            pltpu.VMEM((n_rows, features), BF16),
            pltpu.VMEM((n_ctx, n_rows, features), BF16),
            pltpu.VMEM((n_head, n_sum, cols), F32),
            pltpu.VMEM((n_head, n_sum, cols), F32),
            pltpu.VMEM((n_sum, cols), BF16),
            pltpu.VMEM((n_all, n_sum, cols), BF16),
            pltpu.VMEM((parts, n_all, rows_here, width // parts), BF16),
            pltpu.VMEM((parts, n_all, rows_here, width // parts), BF16),
            pltpu.VMEM((expert_lists.shape[0], LANES), F32),
            pltpu.VMEM((n_all * rows_here, hidden_units), BF16),
            pltpu.VMEM((n_head * n_pair, n_ctx, rows_here, width), F32),
            dma((n_load,)),
            dma((n1,)),
            dma((n1,)),
            dma((n1,)),
            dma((n1,)),
            dma((n_ctx,)),
            dma((n_ctx,)),
            dma((n_head,)),
            dma((n_head,)),
            dma((n_all,)),
            dma((n_all,)),
            dma((parts, n_all)),
            dma((parts, n_all)),
            dma((n_ctx,)),
            dma((n_ctx,)),
        ],
        compiler_params=pltpu.CompilerParams(
            collective_id=0, has_side_effects=True, vmem_limit_bytes=60 * 1024 * 1024
        ),
        name="decode_step",
    )(
        queries,
        residual,
        norm_gain.reshape(1, width),
        expert_lists,
        gate_weights,
        prompt_keys.reshape(flat, LANES),
        prompt_values.reshape(flat, LANES),
        out_weight,
        gate_up,
        down_proj,
    ).astype(BF16)


def solution(mesh):
    in_specs = (
        P("groups", "head", None),
        P(("groups", "ctx", "pair"), "head", None),
        P(("groups", "ctx", "pair"), "head", None),
        P(("groups", "ctx", "head", "pair"), None),
        P("head", "ctx"),
        P(),
        P(("groups", "ctx"), None),
        P(("groups", "ctx"), None),
        P(("ctx", "head", "pair"), None, None),
        P(("ctx", "head", "pair"), None, None),
    )
    out_specs = P(("groups", "ctx", "head", "pair"), None)
    return jax.shard_map(body, mesh=mesh, in_specs=in_specs, out_specs=out_specs, check_vma=False)
```
